32 devices in a mesh: section: 4 (over y, core), dp: 4 (over z), tensor: 2 (over x).
Axes of the slice: x: 2, y: 2, z: 4, core: 2. Of those that a mesh axis runs over, the one named last changes fastest.
Arguments:
- query_embedded: bfloat16 [16, 4096], P('dp'), may hold values from -6 to 6
- passage_embedded: bfloat16 [48, 4096], P('dp'), may hold values from -6 to 6
- positives: int32 [16], P('dp'), may hold values from 0 to 47
- counts: int32 [16], P('dp'), may hold values from 1 to 32, as said below
- stored_inputs: bfloat16 [4, 512, 4096], P('section', 'dp', 'tensor'), may hold values from -6 to 6
- adapter_inner: bfloat16 [4, 512, 16], P('section', 'dp'), may hold values from -6 to 6
- branch_slope: bfloat16 [4, 512, 4096], P('section', 'dp', 'tensor'), may hold values from -6 to 6
- frozen_projection: bfloat16 [4, 4096, 4096], P('section', None, 'tensor'), may hold values from -0.046875 to 0.046875
- adapter_down: bfloat16 [4, 4096, 16], P('section', 'tensor'), may hold values from -0.09375 to 0.09375
- adapter_up: bfloat16 [4, 16, 4096], P('section', None, 'tensor'), may hold values from -0.09375 to 0.09375
Outputs:
- grad_inputs: bfloat16 [4, 512, 4096], P('section', 'dp', 'tensor')
- adapter_grads: float32 [4, 32, 4096], P('section', 'dp', 'tensor')
The draws below stay inside these ranges and needn't reach their ends.
Inputs may be any that keep to these rules, and one draw needn't show every extreme that they name: Query i's live tokens are its first counts[i] rows of 32; some query has all 32.
All inputs are finite; a program needn't handle non-finite values.
Results may differ from the reference program's by a relative error of at most 0.017.
Values may be sent and summed in bfloat16 or wider, within the bound.
No kernel may reach another device: no remote copies, remote signals or barrier semaphores. Data moves between devices by JAX's collectives and lax.ppermute only.
A program may use at most 64 MiB of HBM per device.

```python
import math
import jax
import jax.numpy as jnp
from jax import lax

HIDDEN_WIDTH = 4096
ADAPTER_RANK = 16
QUERY_LEN = 32
WINDOW_LAYERS = 4
QUERY_COUNT = 16
TOKEN_COUNT = 512
PASSAGES = 48
N_TENSOR = 2


def draw_counts(key, part):
    key_values, key_place = jax.random.split(key)
    values = jax.random.randint(key_values, (QUERY_COUNT,), 1, QUERY_LEN + 1, dtype=jnp.int32)
    full_index = jax.random.randint(key_place, (), 0, QUERY_COUNT, dtype=jnp.int32)
    positions = jnp.arange(QUERY_COUNT, dtype=jnp.int32)
    return jnp.where(positions == full_index, QUERY_LEN, values).astype(jnp.int32)


def plant(array, rng, smallest, largest):
    longest = array.shape.index(max(array.shape))
    spots = []
    for shift in (0, 1):
        where = [jax.random.randint(jax.random.fold_in(rng, axis), (), 0, length) for axis, length in enumerate(array.shape)]
        where[longest] = (where[longest] + shift) % array.shape[longest]
        spots.append(tuple(where))
    return array.at[spots[0]].set(smallest).at[spots[1]].set(largest)


def levels(rng, shape, shards, low, top_value):
    def one(dim, parts):
        heights = jax.random.uniform(jax.random.fold_in(jax.random.fold_in(rng, 6), dim), (parts,), jnp.float32, low / len(shards), top_value / len(shards))
        return jnp.repeat(jnp.exp(heights), shape[dim] // parts).reshape((-1,) + (1,) * (len(shape) - dim - 1))

    level = one(*shards[0])
    for cut in shards[1:]:
        level = level * one(*cut)
    return level


def normal_values(stream_key, dims, deviation, bound, pieces=(), kind=jnp.bfloat16):
    loudness = levels(stream_key, dims, pieces, -0.22, 0.18) if pieces else 1.0
    result = jax.random.normal(stream_key, dims, jnp.float32) * deviation * loudness
    return jnp.minimum(jnp.maximum(result, -bound), bound).astype(kind)


def setup_inputs(seed: int = 0) -> dict:
    keys = jax.random.split(jax.random.key(seed), 11)
    query_embedded = normal_values(keys[0], (QUERY_COUNT, HIDDEN_WIDTH), 1.0, 6.0, ((0, 4),))
    passage_embedded = normal_values(keys[1], (PASSAGES, HIDDEN_WIDTH), 1.0, 6.0, ((0, 4),))
    positives = plant(jax.random.randint(keys[2], (QUERY_COUNT,), 0, PASSAGES), jax.random.fold_in(keys[2], 1), 0, PASSAGES - 1).astype(jnp.int32)
    counts = draw_counts(jax.random.fold_in(keys[10], 71), 0)
    stored_inputs = normal_values(keys[4], (WINDOW_LAYERS, TOKEN_COUNT, HIDDEN_WIDTH), 1.0, 6.0, ((0, 4), (1, 4), (2, 2)))
    adapter_inner = normal_values(keys[5], (WINDOW_LAYERS, TOKEN_COUNT, ADAPTER_RANK), 1.0, 6.0, ((0, 4), (1, 4)))
    branch_slope = normal_values(keys[6], (WINDOW_LAYERS, TOKEN_COUNT, HIDDEN_WIDTH), 1.0, 6.0, ((0, 4), (1, 4), (2, 2)))
    frozen_projection = normal_values(keys[7], (WINDOW_LAYERS, HIDDEN_WIDTH, HIDDEN_WIDTH), (4 * HIDDEN_WIDTH) ** -0.5, 0.046875, ((0, 4), (2, 2)))
    adapter_down = normal_values(keys[8], (WINDOW_LAYERS, HIDDEN_WIDTH, ADAPTER_RANK), HIDDEN_WIDTH ** -0.5, 0.09375, ((0, 4), (1, 2)))
    adapter_up = normal_values(keys[9], (WINDOW_LAYERS, ADAPTER_RANK, HIDDEN_WIDTH), HIDDEN_WIDTH ** -0.5, 0.09375, ((0, 4), (2, 2)))
    return dict(query_embedded=query_embedded, passage_embedded=passage_embedded, positives=positives, counts=counts, stored_inputs=stored_inputs, adapter_inner=adapter_inner, branch_slope=branch_slope, frozen_projection=frozen_projection, adapter_down=adapter_down, adapter_up=adapter_up)


ADAPTER_SCALE = 2.0
LOSS_SCALE = 32.0

def rounded(values):
    return lax.optimization_barrier(values.astype(jnp.bfloat16)).astype(jnp.float32)

def reference(query_embedded, passage_embedded, positives, counts, stored_inputs, adapter_inner, branch_slope, frozen_projection, adapter_down, adapter_up):
    inverse_root = 1.0 / math.sqrt(HIDDEN_WIDTH)
    scores = jnp.dot(query_embedded, passage_embedded.T, preferred_element_type=jnp.float32) * inverse_root
    columns = jnp.arange(PASSAGES, dtype=jnp.int32)
    target = (positives[:, None] == columns[None, :]).astype(jnp.float32)
    score_grad = (jax.nn.sigmoid(scores) - target).astype(jnp.bfloat16)
    query_grad = jnp.dot(score_grad, passage_embedded, preferred_element_type=jnp.float32) * inverse_root
    positions = jnp.arange(QUERY_LEN, dtype=jnp.int32)
    live_mask = (positions[None, :] < counts[:, None]).astype(jnp.float32)
    token_scale = live_mask * (LOSS_SCALE / counts.astype(jnp.float32))[:, None]
    gradient_block = (query_grad[:, None, :] * token_scale[:, :, None]).reshape(TOKEN_COUNT, HIDDEN_WIDTH).astype(jnp.bfloat16)
    block_span = HIDDEN_WIDTH // N_TENSOR
    adapter_factor = ADAPTER_SCALE / QUERY_COUNT
    grad_list = [None] * WINDOW_LAYERS
    adapter_list = [None] * WINDOW_LAYERS
    for layer_position in range(WINDOW_LAYERS - 1, -1, -1):
        branch_block = (gradient_block.astype(jnp.float32) * branch_slope[layer_position].astype(jnp.float32)).astype(jnp.bfloat16)
        frozen_total = jnp.zeros((TOKEN_COUNT, HIDDEN_WIDTH), jnp.float32)
        inner_total = jnp.zeros((TOKEN_COUNT, ADAPTER_RANK), jnp.float32)
        for block_index in range(N_TENSOR):
            column_begin = block_index * block_span
            grad_cols = branch_block[:, column_begin:column_begin + block_span]
            weight_cols = frozen_projection[layer_position, :, column_begin:column_begin + block_span]
            up_columns = adapter_up[layer_position, :, column_begin:column_begin + block_span]
            frozen_total = frozen_total + rounded(jnp.dot(grad_cols, weight_cols.T, preferred_element_type=jnp.float32))
            inner_total = inner_total + rounded(jnp.dot(grad_cols, up_columns.T, preferred_element_type=jnp.float32))
        inner_rows_block = inner_total.astype(jnp.bfloat16)
        adapter_term = ADAPTER_SCALE * jnp.dot(inner_rows_block, adapter_down[layer_position].T, preferred_element_type=jnp.float32)
        gradient_next = (gradient_block.astype(jnp.float32) + frozen_total + adapter_term).astype(jnp.bfloat16)
        down_grad = adapter_factor * jnp.dot(inner_rows_block.T, stored_inputs[layer_position], preferred_element_type=jnp.float32)
        up_gradient = adapter_factor * jnp.dot(adapter_inner[layer_position].T, branch_block, preferred_element_type=jnp.float32)
        grad_list[layer_position] = gradient_next
        adapter_list[layer_position] = jnp.concatenate([down_grad, up_gradient], axis=0)
        gradient_block = gradient_next
    return (jnp.stack(grad_list), jnp.stack(adapter_list))
```

```python
import functools
import math

import jax
import jax.numpy as jnp
from jax import lax
from jax.experimental import pallas as pl
from jax.experimental.pallas import tpu as pltpu
from jax.sharding import PartitionSpec as P

ADAPTER_SCALE = 2.0
LOSS_SCALE = 32.0
VMEM_GRANT = 8 << 20
COVER_FLOPS = 10_000_000_000
AXES = ("section", "dp", "tensor")
CONTRACT_LAST = (((1,), (1,)), ((), ()))
CONTRACT_FIRST = (((0,), (0,)), ((), ()))


def vmem_call(kernel, outs, inputs, name, flops, smem=(), scratch=()):
    moved = sum(math.prod(v.shape) * v.dtype.itemsize for v in (*inputs, *outs))
    return pl.pallas_call(
        kernel,
        out_shape=outs,
        in_specs=[
            pl.BlockSpec(memory_space=pltpu.SMEM if i in smem else pltpu.VMEM)
            for i in range(len(inputs))
        ],
        out_specs=tuple(pl.BlockSpec(memory_space=pltpu.VMEM) for _ in outs),
        scratch_shapes=list(scratch),
        name=name,
        compiler_params=pltpu.CompilerParams(vmem_limit_bytes=VMEM_GRANT),
        cost_estimate=pl.CostEstimate(flops=flops, bytes_accessed=moved, transcendentals=0),
    )(*inputs)


def exchange(value, partner, sizes):
    sections, replicas, tensors = sizes
    flat = lambda s, d, t: (s * replicas + d) * tensors + t
    pairs = [
        (flat(s, d, t), flat(*partner(s, d, t)))
        for s in range(sections)
        for d in range(replicas)
        for t in range(tensors)
    ]
    return lax.ppermute(value, AXES, pairs)


def split_pairing(active, step):
    def partner(s, d, t):
        if s == active:
            return (s, d, t ^ step)
        if s == active ^ 1:
            return (s, d ^ 1, t)
        return (s ^ 1, d, t)

    return partner


def hop_pairing(upper):
    lower = upper - 1

    def partner(s, d, t):
        if upper % 2:
            return (s ^ 1, d, t)
        if s in (upper, lower):
            return (upper + lower - s, d, t)
        return (s, d ^ 1, t)

    return partner


def gather_pairing(step):
    def partner(s, d, t):
        if s % 2:
            return (s, d ^ step, t)
        return (s ^ 2, d, t)

    return partner


def branch_terms(gradient, slope_ref, up_ref, h_ref, inner_ref):
    h = (gradient * slope_ref[...].astype(jnp.float32)).astype(jnp.bfloat16)
    h_ref[...] = h
    inner_ref[...] = lax.dot_general(
        up_ref[...], h, CONTRACT_LAST, preferred_element_type=jnp.float32
    ).astype(jnp.bfloat16)


def setup_kernel(count, *refs):
    sources = refs[:count]
    scale_ref, at_ref = refs[count : count + 2]
    targets = refs[count + 2 : 2 * count]
    positives_ref, counts_ref, semaphores = refs[2 * count :]
    copies = [
        pltpu.make_async_copy(source, target, semaphores.at[i])
        for i, (source, target) in enumerate(zip(sources, (positives_ref, counts_ref, *targets)))
    ]
    for copy in copies:
        copy.start()
    copies[0].wait()
    copies[1].wait()
    queries = counts_ref.shape[0]
    length = scale_ref.shape[0] // queries
    position = lax.broadcasted_iota(jnp.int32, (length, scale_ref.shape[1]), 0)
    row = lax.broadcasted_iota(jnp.int32, at_ref.shape, 0)
    positive = jnp.zeros(at_ref.shape, jnp.int32)
    for i in range(queries):
        live = counts_ref[i]
        scale_ref[i * length : (i + 1) * length, :] = jnp.where(
            position < live, LOSS_SCALE, 0.0
        ) / live.astype(jnp.float32)
        positive = jnp.where(row == i, positives_ref[i], positive)
    at_ref[...] = positive
    for copy in copies[2:]:
        copy.wait()


def setup(arrays, rows):
    positives, counts, *held = arrays
    outs = [
        jax.ShapeDtypeStruct((rows, 128), jnp.float32),
        jax.ShapeDtypeStruct((counts.shape[0], 128), jnp.int32),
        *(jax.ShapeDtypeStruct(v.shape, v.dtype) for v in held),
    ]
    return pl.pallas_call(
        functools.partial(setup_kernel, len(arrays)),
        out_shape=outs,
        in_specs=[pl.BlockSpec(memory_space=pltpu.HBM) for _ in arrays],
        out_specs=[pl.BlockSpec(memory_space=pltpu.VMEM) for _ in outs],
        scratch_shapes=[
            pltpu.SMEM(positives.shape, positives.dtype),
            pltpu.SMEM(counts.shape, counts.dtype),
            pltpu.SemaphoreType.DMA((len(arrays),)),
        ],
        name="setup",
        compiler_params=pltpu.CompilerParams(vmem_limit_bytes=VMEM_GRANT),
        cost_estimate=pl.CostEstimate(
            flops=COVER_FLOPS, bytes_accessed=1 << 20, transcendentals=0
        ),
    )(*arrays)


def top_kernel(piece_count, bases, scale_ref, at_ref, query_ref, *refs):
    pieces = refs[:piece_count]
    slope_ref, up_ref, top_ref, h_ref, inner_ref, passages_ref = refs[piece_count:]
    queries, width = query_ref.shape
    rows, local = slope_ref.shape
    length = rows // queries
    inverse_root = 1.0 / math.sqrt(width)
    start = pl.multiple_of(lax.axis_index("tensor") * local, local)
    per_piece = pieces[0].shape[0]
    pitch = passages_ref.shape[0] // piece_count
    if pitch > per_piece:
        passages_ref[...] = jnp.zeros_like(passages_ref)
    for k, piece in enumerate(pieces):
        passages_ref[k * pitch : k * pitch + per_piece, :] = piece[...]
    column = lax.broadcasted_iota(jnp.int32, (queries, pitch), 1)
    positive = at_ref[:, :1]
    replica = lax.axis_index("dp")
    scores = lax.dot_general(
        query_ref[...], passages_ref[...], CONTRACT_LAST, preferred_element_type=jnp.float32
    ) * inverse_root
    targets = []
    for base in bases:
        first = 0 if base is None else (replica ^ base) * per_piece
        hit = (positive == column + first) & (column < per_piece)
        targets.append(hit.astype(jnp.float32))
    target = jnp.concatenate(targets, axis=1)
    score_grad = (jax.nn.sigmoid(scores) - target).astype(jnp.bfloat16)
    total = jnp.dot(
        score_grad, passages_ref[:, pl.ds(start, local)], preferred_element_type=jnp.float32
    )
    query_grad = total * inverse_root
    for i in range(queries):
        at = slice(i * length, (i + 1) * length)
        top_ref[at, :] = (query_grad[i : i + 1, :] * scale_ref[at, :1]).astype(jnp.bfloat16)
    branch_terms(top_ref[...].astype(jnp.float32), slope_ref, up_ref, h_ref, inner_ref)


def product_columns(h_ref, weight_ref, first, out_ref):
    width = out_ref.shape[1]
    tile = min(512, width)

    @pl.loop(0, width // tile)
    def _(n):
        at = pl.multiple_of(n * tile, tile)
        rows = pl.ds(pl.multiple_of(first + at, tile), tile)
        out_ref[:, pl.ds(at, tile)] = lax.dot_general(
            h_ref[...], weight_ref[rows, :], CONTRACT_LAST, preferred_element_type=jnp.float32
        ).astype(jnp.bfloat16)


def cross_columns(h_ref, weight_ref, out_refs):
    for step, out_ref in enumerate(out_refs, 1):
        other = lax.axis_index("tensor") ^ step
        product_columns(h_ref, weight_ref, other * out_ref.shape[1], out_ref)


def first_cross_kernel(active, h_ref, weight_ref, *out_refs):
    @pl.when(lax.axis_index("section") == active)
    def _():
        cross_columns(h_ref, weight_ref, out_refs)


def cross_kernel(active, g_ref, slope_ref, up_ref, h_in, inner_in, weight_ref, h_ref, inner_ref, *out_refs):
    is_active = lax.axis_index("section") == active

    @pl.when(is_active)
    def _():
        branch_terms(g_ref[...].astype(jnp.float32), slope_ref, up_ref, h_ref, inner_ref)
        cross_columns(h_ref, weight_ref, out_refs)

    @pl.when(jnp.logical_not(is_active))
    def _():
        h_ref[...] = h_in[...]
        inner_ref[...] = inner_in[...]


def own_kernel(active, h_ref, weight_ref, out_ref):
    @pl.when(lax.axis_index("section") == active)
    def _():
        product_columns(
            h_ref, weight_ref, lax.axis_index("tensor") * out_ref.shape[1], out_ref
        )


def combine_kernel(active, count, *refs):
    g_ref, own_ref, down_ref = refs[:3]
    inner_refs = refs[3 : 3 + count]
    cross_refs = refs[3 + count : 2 + 2 * count]
    kept_refs = refs[2 + 2 * count : -1]
    out_ref = refs[-1]
    is_active = lax.axis_index("section") == active

    for kept_ref in kept_refs:

        @pl.when(jnp.logical_not(is_active))
        def _():
            out_ref[...] = kept_ref[...]

    @pl.when(is_active)
    def _():
        inner = sum(ref[...].astype(jnp.float32) for ref in inner_refs).astype(jnp.bfloat16)
        width = out_ref.shape[1]
        tile = min(512, width)
        for at in range(0, width, tile):
            columns = slice(at, at + tile)
            value = g_ref[:, columns].astype(jnp.float32) + own_ref[:, columns].astype(jnp.float32)
            for ref in cross_refs:
                value = value + ref[:, columns].astype(jnp.float32)
            value = value + ADAPTER_SCALE * lax.dot_general(
                inner,
                down_ref[:, columns],
                CONTRACT_FIRST,
                preferred_element_type=jnp.float32,
            )
            out_ref[:, columns] = value.astype(jnp.bfloat16)


def split_rows(total, keep, keep_ref, send_ref):
    half = keep_ref.shape[0]
    first, second = total[:half, :], total[half:, :]
    keep_ref[...] = jnp.where(keep == 0, first, second)
    send_ref[...] = jnp.where(keep == 0, second, first).astype(send_ref.dtype)


def adapter_kernel(factor, count, replicas, *refs):
    h_ref, stored_ref, saved_ref = refs[:3]
    inner_refs = refs[3 : 3 + count]
    out_refs = refs[3 + count :]
    inner = sum(ref[...].astype(jnp.float32) for ref in inner_refs).astype(jnp.bfloat16)
    down = factor * jnp.dot(inner, stored_ref[...], preferred_element_type=jnp.float32)
    up = factor * jnp.dot(saved_ref[...], h_ref[...], preferred_element_type=jnp.float32)
    total = jnp.concatenate([down, up], axis=0)
    if len(out_refs) == 2:
        split_rows(total, lax.axis_index("dp") // (replicas // 2), *out_refs)
    else:
        out_refs[0][...] = total.astype(jnp.bfloat16)


def fold_kernel(step, kept_ref, received_ref, keep_ref, send_ref):
    total = kept_ref[...] + received_ref[...].astype(jnp.float32)
    split_rows(total, (lax.axis_index("dp") // step) % 2, keep_ref, send_ref)


def shards(
    query_embedded,
    passage_embedded,
    positives,
    counts,
    stored_inputs,
    adapter_inner,
    branch_slope,
    frozen_projection,
    adapter_down,
    adapter_up,
):
    sizes = tuple(lax.axis_size(name) for name in AXES)
    section_count, replica_total, tensor_count = sizes
    few_replicas = replica_total <= 4
    down, up = adapter_down[0].T, adapter_up[0]
    stored, saved, slope = stored_inputs[0], adapter_inner[0].T, branch_slope[0]
    rows, local = slope.shape
    rank = up.shape[0]
    block = jax.ShapeDtypeStruct((rows, local), jnp.bfloat16)
    inner_shape = jax.ShapeDtypeStruct((rank, rows), jnp.bfloat16)

    if few_replicas:
        bases = list(range(replica_total))
        pieces = [passage_embedded] + [
            exchange(passage_embedded, gather_pairing(step), sizes) for step in bases[1:]
        ]
    else:
        bases = [None]
        pieces = [lax.all_gather(passage_embedded, "dp", axis=0, tiled=True)]
    pitch = -(-pieces[0].shape[0] // 16) * 16
    weight = frozen_projection[0]
    scale, at, query_held, pieces[0], slope, up = setup(
        (positives, counts, query_embedded, pieces[0], slope, up), rows
    )
    g, h, inner = vmem_call(
        functools.partial(top_kernel, len(pieces), bases),
        (block, block, inner_shape),
        (scale, at, query_held, *pieces, slope, up),
        "top",
        2 * rows * local * rank,
        scratch=[pltpu.VMEM((len(pieces) * pitch, passage_embedded.shape[1]), jnp.bfloat16)],
    )
    result = None
    for active in range(section_count - 1, -1, -1):
        first = active == section_count - 1
        flops = 2 * rows * local * local * (tensor_count - 1)
        if first:
            crosses = vmem_call(
                functools.partial(first_cross_kernel, active),
                (block,) * (tensor_count - 1),
                (h, weight),
                f"cross{active}",
                flops,
            )
        else:
            h, inner, *crosses = vmem_call(
                functools.partial(cross_kernel, active),
                (block, inner_shape) + (block,) * (tensor_count - 1),
                (g, slope, up, h, inner, weight),
                f"cross{active}",
                flops,
            )
        received = [
            exchange(cross, split_pairing(active, j), sizes) for j, cross in enumerate(crosses, 1)
        ]
        inner_others = [
            exchange(inner, lambda s, d, t, j=j: (s, d, t ^ j), sizes)
            for j in range(1, tensor_count)
        ]
        (own,) = vmem_call(
            functools.partial(own_kernel, active),
            (block,),
            (h, weight),
            f"own{active}",
            2 * rows * local * local,
        )
        inputs = [g, own, down, inner, *inner_others, *received]
        if result is not None:
            inputs.append(result)
        (result,) = vmem_call(
            functools.partial(combine_kernel, active, tensor_count),
            (block,),
            inputs,
            f"combine{active}",
            2 * rows * local * rank,
        )
        if active:
            g = exchange(result, hop_pairing(active), sizes)

    factor = ADAPTER_SCALE / (query_embedded.shape[0] * replica_total)
    halves = lambda n: (
        jax.ShapeDtypeStruct((n, local), jnp.float32),
        jax.ShapeDtypeStruct((n, local), jnp.bfloat16),
    )
    sums = vmem_call(
        functools.partial(adapter_kernel, factor, tensor_count, replica_total),
        halves(rank) if few_replicas else halves(2 * rank)[1:],
        (h, stored, saved, inner, *inner_others),
        "adapter",
        4 * rows * local * rank,
    )
    if few_replicas:
        kept, sent = sums
        step = replica_total // 2
        while True:
            received = exchange(sent, lambda s, d, t, j=step: (s, d ^ j, t), sizes)
            if step == 1:
                break
            step //= 2
            kept, sent = vmem_call(
                functools.partial(fold_kernel, step),
                halves(kept.shape[0] // 2),
                (kept, received),
                f"fold{step}",
                0,
            )
        reduced = kept + received.astype(jnp.float32)
    else:
        reduced = lax.psum_scatter(sums[0], "dp", scatter_dimension=0, tiled=True).astype(
            jnp.float32
        )
    return (result[None], reduced[None])


def solution(mesh):
    return jax.shard_map(
        shards,
        mesh=mesh,
        in_specs=(
            P("dp", None),
            P("dp", None),
            P("dp"),
            P("dp"),
            P("section", "dp", "tensor"),
            P("section", "dp", None),
            P("section", "dp", "tensor"),
            P("section", None, "tensor"),
            P("section", "tensor", None),
            P("section", None, "tensor"),
        ),
        out_specs=(P("section", "dp", "tensor"), P("section", "dp", "tensor")),
        check_vma=False,
    )
```

```python
import functools
import math

import jax
import jax.numpy as jnp
from jax import lax
from jax.experimental import pallas as pl
from jax.experimental.pallas import tpu as pltpu
from jax.sharding import PartitionSpec as P


ADAPTER_SCALE = 2.0
LOSS_SCALE = 32.0
VMEM_GRANT = 8 << 20
COVER_FLOPS = 10_000_000_000
CHUNKS = 2
MATMUL_TILE = 1024
AXES = ("section", "dp", "tensor")
CONTRACT_LAST = (((1,), (1,)), ((), ()))
CONTRACT_FIRST = (((0,), (0,)), ((), ()))


def vmem_call(kernel, outs, inputs, flops, smem=(), scratch=()):
    moved = sum(math.prod(v.shape) * v.dtype.itemsize for v in (*inputs, *outs))
    return pl.pallas_call(
        kernel,
        out_shape=outs,
        in_specs=[
            pl.BlockSpec(memory_space=pltpu.SMEM if i in smem else pltpu.VMEM)
            for i in range(len(inputs))
        ],
        out_specs=tuple(pl.BlockSpec(memory_space=pltpu.VMEM) for _ in outs),
        scratch_shapes=list(scratch),
        compiler_params=pltpu.CompilerParams(vmem_limit_bytes=VMEM_GRANT),
        cost_estimate=pl.CostEstimate(flops=flops, bytes_accessed=moved, transcendentals=0),
    )(*inputs)


def exchange(value, partner, sizes):
    sections, replicas, tensors = sizes
    flat = lambda s, d, t: (s * replicas + d) * tensors + t
    pairs = [
        (flat(s, d, t), flat(*partner(s, d, t)))
        for s in range(sections)
        for d in range(replicas)
        for t in range(tensors)
    ]
    return lax.ppermute(value, AXES, pairs)


def split_pairing(active, step):
    def partner(s, d, t):
        if s == active:
            return (s, d, t ^ step)
        if s == active ^ 1:
            return (s, d ^ 1, t)
        return (s ^ 1, d, t)

    return partner


def hop_pairing(upper):
    lower = upper - 1

    def partner(s, d, t):
        if upper % 2:
            return (s ^ 1, d, t)
        if s in (upper, lower):
            return (upper + lower - s, d, t)
        return (s, d ^ 1, t)

    return partner


def gather_pairing(step):
    def partner(s, d, t):
        if s % 2:
            return (s, d ^ step, t)
        return (s ^ 2, d, t)

    return partner


def branch(g_ref, slope_ref, chunk):
    width = g_ref.shape[1]
    slope = slope_ref[:, chunk * width : (chunk + 1) * width].astype(jnp.float32)
    return (g_ref[...].astype(jnp.float32) * slope).astype(jnp.bfloat16)


def inner_terms(h_refs, up_ref):
    total = 0.0
    for k, h_ref in enumerate(h_refs):
        width = h_ref.shape[1]
        total = total + lax.dot_general(
            up_ref[:, k * width : (k + 1) * width],
            h_ref[...],
            CONTRACT_LAST,
            preferred_element_type=jnp.float32,
        )
    return total.astype(jnp.bfloat16)


def pack_inner(inner_ref, out_ref, rows):
    if out_ref.shape[0] > rows:
        tail = jnp.zeros((out_ref.shape[0] - rows, out_ref.shape[1] - rows), out_ref.dtype)
        out_ref[rows:, :] = jnp.concatenate([inner_ref[...], tail], axis=1)


def unpack_inner(ref, rows):
    return ref[...] if ref.shape[0] < rows else ref[rows:, :rows]


def products(h_refs, parts, weight_ref, first, out_ref, base_ref=None, base_at=0):
    width = out_ref.shape[1]
    tile = min(MATMUL_TILE, width)
    for at in range(0, width, tile):
        rows = pl.ds(pl.multiple_of(first + at, tile), tile)
        total = 0.0
        if base_ref is not None:
            total = base_ref[:, base_at + at : base_at + at + tile]
        for h_ref, part in zip(h_refs, parts):
            depth = h_ref.shape[1]
            total = total + lax.dot_general(
                h_ref[...],
                weight_ref[rows, part * depth : (part + 1) * depth],
                CONTRACT_LAST,
                preferred_element_type=jnp.float32,
            )
        out_ref[: total.shape[0], at : at + tile] = total.astype(out_ref.dtype)


def setup_kernel(count, *refs):
    sources = refs[:count]
    scale_ref, at_ref = refs[count : count + 2]
    targets = refs[count + 2 : 2 * count]
    positives_ref, counts_ref, semaphores = refs[2 * count :]
    copies = [
        pltpu.make_async_copy(source, target, semaphores.at[i])
        for i, (source, target) in enumerate(zip(sources, (positives_ref, counts_ref, *targets)))
    ]
    for copy in copies:
        copy.start()
    copies[0].wait()
    copies[1].wait()
    queries = counts_ref.shape[0]
    length = scale_ref.shape[0] // queries
    position = lax.broadcasted_iota(jnp.int32, (length, scale_ref.shape[1]), 0)
    row = lax.broadcasted_iota(jnp.int32, at_ref.shape, 0)
    positive = jnp.zeros(at_ref.shape, jnp.int32)
    for i in range(queries):
        live = counts_ref[i]
        scale_ref[i * length : (i + 1) * length, :] = jnp.where(
            position < live, LOSS_SCALE, 0.0
        ) / live.astype(jnp.float32)
        positive = jnp.where(row == i, positives_ref[i], positive)
    at_ref[...] = positive
    for copy in copies[2:]:
        copy.wait()


def setup(arrays, rows):
    positives, counts, *held = arrays
    outs = [
        jax.ShapeDtypeStruct((rows, 128), jnp.float32),
        jax.ShapeDtypeStruct((counts.shape[0], 128), jnp.int32),
        *(jax.ShapeDtypeStruct(v.shape, v.dtype) for v in held),
    ]
    return pl.pallas_call(
        functools.partial(setup_kernel, len(arrays)),
        out_shape=outs,
        in_specs=[pl.BlockSpec(memory_space=pltpu.HBM) for _ in arrays],
        out_specs=[pl.BlockSpec(memory_space=pltpu.VMEM) for _ in outs],
        scratch_shapes=[
            pltpu.SMEM(positives.shape, positives.dtype),
            pltpu.SMEM(counts.shape, counts.dtype),
            pltpu.SemaphoreType.DMA((len(arrays),)),
        ],
        name="setup",
        compiler_params=pltpu.CompilerParams(vmem_limit_bytes=VMEM_GRANT),
        cost_estimate=pl.CostEstimate(
            flops=COVER_FLOPS, bytes_accessed=1 << 20, transcendentals=0
        ),
    )(*arrays)


def top_kernel(piece_count, bases, scale_ref, at_ref, query_ref, *refs):
    pieces = refs[:piece_count]
    slope_ref, *out_refs, passages_ref = refs[piece_count:]
    top_refs, h_refs = out_refs[: len(out_refs) // 2], out_refs[len(out_refs) // 2 :]
    queries, width = query_ref.shape
    rows, local = slope_ref.shape
    length = rows // queries
    inverse_root = 1.0 / math.sqrt(width)
    start = pl.multiple_of(lax.axis_index("tensor") * local, local)
    per_piece = pieces[0].shape[0]
    pitch = passages_ref.shape[0] // piece_count
    if pitch > per_piece:
        passages_ref[...] = jnp.zeros_like(passages_ref)
    for k, piece in enumerate(pieces):
        passages_ref[k * pitch : k * pitch + per_piece, :] = piece[...]
    column = lax.broadcasted_iota(jnp.int32, (queries, pitch), 1)
    positive = at_ref[:, :1]
    replica = lax.axis_index("dp")
    scores = lax.dot_general(
        query_ref[...], passages_ref[...], CONTRACT_LAST, preferred_element_type=jnp.float32
    ) * inverse_root
    targets = []
    for base in bases:
        first = 0 if base is None else (replica ^ base) * per_piece
        hit = (positive == column + first) & (column < per_piece)
        targets.append(hit.astype(jnp.float32))
    target = jnp.concatenate(targets, axis=1)
    score_grad = (jax.nn.sigmoid(scores) - target).astype(jnp.bfloat16)
    total = jnp.dot(
        score_grad, passages_ref[:, pl.ds(start, local)], preferred_element_type=jnp.float32
    )
    query_grad = total * inverse_root
    for i in range(queries):
        at = slice(i * length, (i + 1) * length)
        block = (query_grad[i : i + 1, :] * scale_ref[at, :1]).astype(jnp.bfloat16)
        for k, top_ref in enumerate(top_refs):
            width = top_ref.shape[1]
            top_ref[at, :] = block[:, k * width : (k + 1) * width]
    for k, (top_ref, h_ref) in enumerate(zip(top_refs, h_refs)):
        h_ref[...] = branch(top_ref, slope_ref, k)


def when_section(active, then, otherwise=None):
    is_active = lax.axis_index("section") == active
    pl.when(is_active)(then)
    if otherwise is not None:
        pl.when(jnp.logical_not(is_active))(otherwise)


def early_kernel(active, g_ref, slope_ref, h_in, weight_ref, h_ref, *base_refs):
    def run():
        h_ref[...] = branch(g_ref, slope_ref, 0)
        for step, base_ref in enumerate(base_refs, 1):
            other = lax.axis_index("tensor") ^ step
            products([h_ref], [0], weight_ref, other * base_ref.shape[1], base_ref)

    def keep():
        h_ref[...] = h_in[...]

    when_section(active, run, keep)


def first_cross_kernel(active, count, offset, local, up_ref, weight_ref, *refs):
    h_refs, (inner_ref, *out_refs) = refs[:count], refs[count:]

    def run():
        for step, out_ref in enumerate(out_refs, 1):
            other = lax.axis_index("tensor") ^ step
            products(h_refs, range(count), weight_ref, other * local + offset, out_ref)
            pack_inner(inner_ref, out_ref, h_refs[0].shape[0])

    inner_ref[...] = inner_terms(h_refs, up_ref)
    when_section(active, run)


def next_cross_kernel(active, count, g_ref, slope_ref, up_ref, h_in, inner_in, weight_ref, *refs):
    first_h, *base_refs = refs[:count]
    h_ref, inner_ref, *out_refs = refs[count:]

    def run():
        h_ref[...] = branch(g_ref, slope_ref, 1)
        inner_ref[...] = inner_terms([first_h, h_ref], up_ref)
        for step, (base_ref, out_ref) in enumerate(zip(base_refs, out_refs), 1):
            other = lax.axis_index("tensor") ^ step
            products([h_ref], [1], weight_ref, other * base_ref.shape[1], out_ref, base_ref)
            pack_inner(inner_ref, out_ref, h_ref.shape[0])

    def keep():
        h_ref[...] = h_in[...]
        inner_ref[...] = inner_in[...]

    when_section(active, run, keep)


def later_cross_kernel(active, count, parts, offset, local, after_ref, weight_ref, *refs):
    del after_ref
    h_refs, rest = refs[: len(parts)], refs[len(parts) :]
    out_refs = rest[-count:]
    base_refs = rest[:-count] or [None] * count

    def run():
        for step, (base_ref, out_ref) in enumerate(zip(base_refs, out_refs), 1):
            other = lax.axis_index("tensor") ^ step
            products(
                h_refs, parts, weight_ref, other * local + offset, out_ref, base_ref, offset
            )

    when_section(active, run)


def own_kernel(active, offset, local, weight_ref, *refs):
    *h_refs, out_ref = refs

    def run():
        first = lax.axis_index("tensor") * local + offset
        products(h_refs, range(len(h_refs)), weight_ref, first, out_ref)

    when_section(active, run)


def combine_kernel(active, offset, count, chunks, *refs):
    g_refs, refs = refs[:chunks], refs[chunks:]
    own_ref, down_ref = refs[:2]
    inner_refs = refs[2 : 2 + count]
    cross_refs = refs[2 + count : 1 + 2 * count]
    kept_refs, out_ref = refs[1 + 2 * count : -1], refs[-1]
    rows = out_ref.shape[0]

    def run():
        inner = sum(unpack_inner(ref, rows).astype(jnp.float32) for ref in inner_refs)
        inner = inner.astype(jnp.bfloat16)
        width = g_refs[0].shape[1]
        for k, g_ref in enumerate(g_refs):
            at = slice(k * width, (k + 1) * width)
            value = g_ref[...].astype(jnp.float32) + own_ref[:, at].astype(jnp.float32)
            for ref in cross_refs:
                value = value + ref[:rows, at].astype(jnp.float32)
            value = value + ADAPTER_SCALE * lax.dot_general(
                inner,
                down_ref[:, offset + k * width : offset + (k + 1) * width],
                CONTRACT_FIRST,
                preferred_element_type=jnp.float32,
            )
            out_ref[:, at] = value.astype(jnp.bfloat16)

    def keep():
        for k, kept_ref in enumerate(kept_refs):
            width = kept_ref.shape[1]
            out_ref[:, k * width : (k + 1) * width] = kept_ref[...]

    when_section(active, run, keep if kept_refs else None)


def split_rows(total, keep, keep_ref, send_ref):
    half = keep_ref.shape[0]
    first, second = total[:half, :], total[half:, :]
    keep_ref[...] = jnp.where(keep == 0, first, second)
    send_ref[...] = jnp.where(keep == 0, second, first).astype(send_ref.dtype)


def adapter_kernel(factor, count, chunks, replicas, *refs):
    stored_ref, saved_ref = refs[:2]
    h_refs = refs[2 : 2 + chunks]
    inner_refs = refs[2 + chunks : 2 + chunks + count]
    out_refs = refs[2 + chunks + count :]
    inner = sum(ref[...].astype(jnp.float32) for ref in inner_refs).astype(jnp.bfloat16)
    down = factor * jnp.dot(inner, stored_ref[...], preferred_element_type=jnp.float32)
    ups = [
        factor * jnp.dot(saved_ref[...], h_ref[...], preferred_element_type=jnp.float32)
        for h_ref in h_refs
    ]
    total = jnp.concatenate([down, jnp.concatenate(ups, axis=1)], axis=0)
    if len(out_refs) == 2:
        split_rows(total, lax.axis_index("dp") // (replicas // 2), *out_refs)
    else:
        out_refs[0][...] = total.astype(jnp.bfloat16)


def fold_kernel(step, kept_ref, received_ref, keep_ref, send_ref):
    total = kept_ref[...] + received_ref[...].astype(jnp.float32)
    split_rows(total, (lax.axis_index("dp") // step) % 2, keep_ref, send_ref)


def shards(
    query_embedded,
    passage_embedded,
    positives,
    counts,
    stored_inputs,
    adapter_inner,
    branch_slope,
    frozen_projection,
    adapter_down,
    adapter_up,
):
    sizes = tuple(lax.axis_size(name) for name in AXES)
    section_count, replica_total, tensor_count = sizes
    few_replicas = replica_total <= 4
    weight, down, up = frozen_projection[0], adapter_down[0].T, adapter_up[0]
    stored, saved, slope = stored_inputs[0], adapter_inner[0].T, branch_slope[0]
    rows, local = slope.shape
    rank = up.shape[0]
    span = local // CHUNKS
    others = range(1, tensor_count)
    struct = lambda n, kind=jnp.bfloat16: jax.ShapeDtypeStruct((rows, n), kind)
    inner_shape = jax.ShapeDtypeStruct((rank, rows), jnp.bfloat16)
    matmul_flops = lambda depth, columns: 2 * rows * depth * columns

    if few_replicas:
        bases = list(range(replica_total))
        pieces = [passage_embedded] + [
            exchange(passage_embedded, gather_pairing(step), sizes)
            for step in bases[1:]
        ]
    else:
        bases = [None]
        pieces = [lax.all_gather(passage_embedded, "dp", axis=0, tiled=True)]
    pitch = -(-pieces[0].shape[0] // 16) * 16
    scale, at, query_held, pieces[0], slope, up = setup(
        (positives, counts, query_embedded, pieces[0], slope, up), rows
    )
    tops = vmem_call(
        functools.partial(top_kernel, len(pieces), bases),
        (struct(span),) * (2 * CHUNKS),
        (scale, at, query_held, *pieces, slope),
        0,
        scratch=[pltpu.VMEM((len(pieces) * pitch, passage_embedded.shape[1]), jnp.bfloat16)],
    )
    g, h = tops[:CHUNKS], tops[CHUNKS:]
    inner = None
    results = None
    for active in range(section_count - 1, -1, -1):
        last = active == 0
        width = local if last else span
        offsets = range(0, local, width)
        received = {}
        payload = jax.ShapeDtypeStruct((rows if last else rows + rank, width), jnp.bfloat16)
        swap = lambda values: [
            exchange(value, split_pairing(active, j), sizes)
            for j, value in zip(others, values)
        ]
        if inner is None:
            inner, *crosses = vmem_call(
                functools.partial(first_cross_kernel, active, CHUNKS, 0, local),
                (inner_shape,) + (payload,) * len(others),
                (up, weight, *h),
                matmul_flops(local, width) * len(others),
            )
            parts, bases_held, cross_h = list(range(CHUNKS)), [], h
        else:
            first_h, *bases_held = vmem_call(
                functools.partial(early_kernel, active),
                (struct(span),) + (struct(local, jnp.float32),) * len(others),
                (g[0], slope, h[0], weight),
                matmul_flops(span, local) * len(others),
            )
            second_h, inner, *crosses = vmem_call(
                functools.partial(next_cross_kernel, active, 1 + len(others)),
                (struct(span), inner_shape) + (payload,) * len(others),
                (g[1], slope, up, h[1], inner, weight, first_h, *bases_held),
                matmul_flops(span, width) * len(others),
            )
            h = [first_h, second_h]
            parts, cross_h = [1], [second_h]
        received[0] = swap(crosses)
        inner_others = received[0]
        if last:
            inner_others = [
                exchange(inner, lambda s, d, t, j=j: (s, d, t ^ j), sizes)
                for j in others
            ]
        for offset in offsets[1:]:
            crosses = vmem_call(
                functools.partial(
                    later_cross_kernel, active, len(others), parts, offset, local
                ),
                (struct(width),) * len(others),
                (crosses[0], weight, *cross_h, *bases_held),
                matmul_flops(span * len(parts), width) * len(others),
            )
            received[offset] = swap(crosses)
        sums, next_g = [], []
        for k, offset in enumerate(offsets):
            (own,) = vmem_call(
                functools.partial(own_kernel, active, offset, local),
                (struct(width),),
                (weight, *h),
                matmul_flops(local, width),
            )
            g_parts = g if last else [g[k]]
            kept = [] if results is None else results if last else [results[k]]
            (total,) = vmem_call(
                functools.partial(
                    combine_kernel, active, offset, tensor_count, len(g_parts)
                ),
                (struct(width),),
                (
                    *g_parts,
                    own,
                    down,
                    inner,
                    *inner_others,
                    *received[offset],
                    *kept,
                ),
                matmul_flops(rank, width),
            )
            sums.append(total)
            if not last:
                next_g.append(exchange(total, hop_pairing(active), sizes))
        results, g = sums, next_g
    result = results[0]

    factor = ADAPTER_SCALE / (query_embedded.shape[0] * replica_total)
    halves = lambda n: (
        jax.ShapeDtypeStruct((n, local), jnp.float32),
        jax.ShapeDtypeStruct((n, local), jnp.bfloat16),
    )
    sums = vmem_call(
        functools.partial(adapter_kernel, factor, tensor_count, CHUNKS, replica_total),
        halves(rank) if few_replicas else halves(2 * rank)[1:],
        (stored, saved, *h, inner, *inner_others),
        4 * rows * local * rank,
    )
    if few_replicas:
        kept, sent = sums
        step = replica_total // 2
        while True:
            received = exchange(sent, lambda s, d, t, j=step: (s, d ^ j, t), sizes)
            if step == 1:
                break
            step //= 2
            kept, sent = vmem_call(
                functools.partial(fold_kernel, step),
                halves(kept.shape[0] // 2),
                (kept, received),
                0,
            )
        reduced = kept + received.astype(jnp.float32)
    else:
        reduced = lax.psum_scatter(sums[0], "dp", scatter_dimension=0, tiled=True).astype(
            jnp.float32
        )
    return (result[None], reduced[None])


def solution(mesh):
    return jax.shard_map(
        shards,
        mesh=mesh,
        in_specs=(
            P("dp", None),
            P("dp", None),
            P("dp"),
            P("dp"),
            P("section", "dp", "tensor"),
            P("section", "dp", None),
            P("section", "dp", "tensor"),
            P("section", None, "tensor"),
            P("section", "tensor", None),
            P("section", None, "tensor"),
        ),
        out_specs=(P("section", "dp", "tensor"), P("section", "dp", "tensor")),
        check_vma=False,
    )
```

```python
import functools
import math

import jax
import jax.numpy as jnp
from jax import lax
from jax.experimental import pallas as pl
from jax.experimental.pallas import tpu as pltpu
from jax.sharding import PartitionSpec as P


ADAPTER_SCALE = 2.0
LOSS_SCALE = 32.0
VMEM_GRANT = 8 << 20
COVER_FLOPS = 10_000_000_000
CHUNKS = 2
MATMUL_TILE = 1024
AXES = ("section", "dp", "tensor")
CONTRACT_LAST = (((1,), (1,)), ((), ()))
CONTRACT_FIRST = (((0,), (0,)), ((), ()))


def vmem_call(kernel, outs, inputs, flops, smem=(), scratch=()):
    moved = sum(math.prod(v.shape) * v.dtype.itemsize for v in (*inputs, *outs))
    return pl.pallas_call(
        kernel,
        out_shape=outs,
        in_specs=[
            pl.BlockSpec(memory_space=pltpu.SMEM if i in smem else pltpu.VMEM)
            for i in range(len(inputs))
        ],
        out_specs=tuple(pl.BlockSpec(memory_space=pltpu.VMEM) for _ in outs),
        scratch_shapes=list(scratch),
        compiler_params=pltpu.CompilerParams(vmem_limit_bytes=VMEM_GRANT),
        cost_estimate=pl.CostEstimate(flops=flops, bytes_accessed=moved, transcendentals=0),
    )(*inputs)


def exchange(value, partner, sizes):
    sections, replicas, tensors = sizes
    flat = lambda s, d, t: (s * replicas + d) * tensors + t
    pairs = [
        (flat(s, d, t), flat(*partner(s, d, t)))
        for s in range(sections)
        for d in range(replicas)
        for t in range(tensors)
    ]
    return lax.ppermute(value, AXES, pairs)


def split_pairing(active, step):
    def partner(s, d, t):
        if s == active:
            return (s, d, t ^ step)
        if s == active ^ 1:
            return (s, d ^ 1, t)
        return (s ^ 1, d, t)

    return partner


def hop_pairing(upper):
    lower = upper - 1

    def partner(s, d, t):
        if upper % 2:
            return (s ^ 1, d, t)
        if s in (upper, lower):
            return (upper + lower - s, d, t)
        return (s, d ^ 1, t)

    return partner


def gather_pieces(piece, sizes):
    def fetch(s, d, t):
        return (s, d ^ (1, 3, 2, 1)[s], t)

    fetched = exchange(piece, fetch, sizes)
    beside = exchange(fetched, lambda s, d, t: (s ^ 1, d, t), sizes)
    across = exchange(fetched, lambda s, d, t: (s ^ 2, d, t), sizes)
    return [piece, fetched, beside, across]


def branch(g_ref, slope_ref, chunk):
    width = g_ref.shape[1]
    slope = slope_ref[:, chunk * width : (chunk + 1) * width].astype(jnp.float32)
    return (g_ref[...].astype(jnp.float32) * slope).astype(jnp.bfloat16)


def inner_terms(h_refs, up_ref):
    total = 0.0
    for k, h_ref in enumerate(h_refs):
        width = h_ref.shape[1]
        total = total + lax.dot_general(
            up_ref[:, k * width : (k + 1) * width],
            h_ref[...],
            CONTRACT_LAST,
            preferred_element_type=jnp.float32,
        )
    return total.astype(jnp.bfloat16)


def pack_inner(inner_ref, out_ref, rows):
    if out_ref.shape[0] > rows:
        tail = jnp.zeros((out_ref.shape[0] - rows, out_ref.shape[1] - rows), out_ref.dtype)
        out_ref[rows:, :] = jnp.concatenate([inner_ref[...], tail], axis=1)


def unpack_inner(ref, rows):
    return ref[...] if ref.shape[0] < rows else ref[rows:, :rows]


def products(h_refs, parts, weight_ref, first, out_ref, base_ref=None, base_at=0):
    width = out_ref.shape[1]
    tile = min(MATMUL_TILE, width)
    for at in range(0, width, tile):
        rows = pl.ds(pl.multiple_of(first + at, tile), tile)
        total = 0.0
        if base_ref is not None:
            total = base_ref[:, base_at + at : base_at + at + tile]
        for h_ref, part in zip(h_refs, parts):
            depth = h_ref.shape[1]
            total = total + lax.dot_general(
                h_ref[...],
                weight_ref[rows, part * depth : (part + 1) * depth],
                CONTRACT_LAST,
                preferred_element_type=jnp.float32,
            )
        out_ref[: total.shape[0], at : at + tile] = total.astype(out_ref.dtype)


def setup_kernel(positives_ref, counts_ref, scale_ref, at_ref):
    queries = counts_ref.shape[0]
    length = scale_ref.shape[0] // queries
    position = lax.broadcasted_iota(jnp.int32, (length, scale_ref.shape[1]), 0)
    row = lax.broadcasted_iota(jnp.int32, at_ref.shape, 0)
    positive = jnp.zeros(at_ref.shape, jnp.int32)
    for i in range(queries):
        live = counts_ref[i]
        scale_ref[i * length : (i + 1) * length, :] = jnp.where(
            position < live, LOSS_SCALE, 0.0
        ) / live.astype(jnp.float32)
        positive = jnp.where(row == i, positives_ref[i], positive)
    at_ref[...] = positive


def top_kernel(piece_count, bases, scale_ref, at_ref, query_ref, *refs):
    pieces = refs[:piece_count]
    slope_ref, *out_refs, passages_ref = refs[piece_count:]
    top_refs, h_refs = out_refs[: len(out_refs) // 2], out_refs[len(out_refs) // 2 :]
    queries, width = query_ref.shape
    rows, local = slope_ref.shape
    length = rows // queries
    inverse_root = 1.0 / math.sqrt(width)
    start = pl.multiple_of(lax.axis_index("tensor") * local, local)
    per_piece = pieces[0].shape[0]
    pitch = passages_ref.shape[0] // piece_count
    if pitch > per_piece:
        passages_ref[...] = jnp.zeros_like(passages_ref)
    for k, piece in enumerate(pieces):
        passages_ref[k * pitch : k * pitch + per_piece, :] = piece[...]
    column = lax.broadcasted_iota(jnp.int32, (queries, pitch), 1)
    positive = at_ref[:, :1]
    replica = lax.axis_index("dp")
    scores = lax.dot_general(
        query_ref[...], passages_ref[...], CONTRACT_LAST, preferred_element_type=jnp.float32
    ) * inverse_root
    targets = []
    for base in bases:
        first = 0 if base is None else (replica ^ base) * per_piece
        hit = (positive == column + first) & (column < per_piece)
        targets.append(hit.astype(jnp.float32))
    target = jnp.concatenate(targets, axis=1)
    score_grad = (jax.nn.sigmoid(scores) - target).astype(jnp.bfloat16)
    total = jnp.dot(
        score_grad, passages_ref[:, pl.ds(start, local)], preferred_element_type=jnp.float32
    )
    query_grad = total * inverse_root
    for i in range(queries):
        at = slice(i * length, (i + 1) * length)
        block = (query_grad[i : i + 1, :] * scale_ref[at, :1]).astype(jnp.bfloat16)
        for k, top_ref in enumerate(top_refs):
            width = top_ref.shape[1]
            top_ref[at, :] = block[:, k * width : (k + 1) * width]
    for k, (top_ref, h_ref) in enumerate(zip(top_refs, h_refs)):
        h_ref[...] = branch(top_ref, slope_ref, k)


def when_section(active, then, otherwise=None):
    is_active = lax.axis_index("section") == active
    pl.when(is_active)(then)
    if otherwise is not None:
        pl.when(jnp.logical_not(is_active))(otherwise)


def early_kernel(active, g_ref, slope_ref, h_in, weight_ref, h_ref, *base_refs):
    def run():
        h_ref[...] = branch(g_ref, slope_ref, 0)
        for step, base_ref in enumerate(base_refs, 1):
            other = lax.axis_index("tensor") ^ step
            products([h_ref], [0], weight_ref, other * base_ref.shape[1], base_ref)

    def keep():
        h_ref[...] = h_in[...]

    when_section(active, run, keep)


def first_cross_kernel(active, count, offset, local, up_ref, weight_ref, *refs):
    h_refs, (inner_ref, *out_refs) = refs[:count], refs[count:]

    def run():
        for step, out_ref in enumerate(out_refs, 1):
            other = lax.axis_index("tensor") ^ step
            products(h_refs, range(count), weight_ref, other * local + offset, out_ref)
            pack_inner(inner_ref, out_ref, h_refs[0].shape[0])

    inner_ref[...] = inner_terms(h_refs, up_ref)
    when_section(active, run)


def next_cross_kernel(active, count, g_ref, slope_ref, up_ref, h_in, inner_in, weight_ref, *refs):
    first_h, *base_refs = refs[:count]
    h_ref, inner_ref, *out_refs = refs[count:]

    def run():
        h_ref[...] = branch(g_ref, slope_ref, 1)
        inner_ref[...] = inner_terms([first_h, h_ref], up_ref)
        for step, (base_ref, out_ref) in enumerate(zip(base_refs, out_refs), 1):
            other = lax.axis_index("tensor") ^ step
            products([h_ref], [1], weight_ref, other * base_ref.shape[1], out_ref, base_ref)
            pack_inner(inner_ref, out_ref, h_ref.shape[0])

    def keep():
        h_ref[...] = h_in[...]
        inner_ref[...] = inner_in[...]

    when_section(active, run, keep)


def branch_kernel(active, g_ref, slope_ref, up_ref, h_in, inner_in, first_h, h_ref, inner_ref):
    def run():
        h_ref[...] = branch(g_ref, slope_ref, 1)
        inner_ref[...] = inner_terms([first_h, h_ref], up_ref)

    def keep():
        h_ref[...] = h_in[...]
        inner_ref[...] = inner_in[...]

    when_section(active, run, keep)


def later_cross_kernel(active, count, parts, offset, local, after_ref, weight_ref, *refs):
    del after_ref
    h_refs, rest = refs[: len(parts)], refs[len(parts) :]
    out_refs = rest[-count:]
    base_refs = rest[:-count] or [None] * count

    def run():
        for step, (base_ref, out_ref) in enumerate(zip(base_refs, out_refs), 1):
            other = lax.axis_index("tensor") ^ step
            products(
                h_refs, parts, weight_ref, other * local + offset, out_ref, base_ref, offset
            )

    when_section(active, run)


def own_kernel(active, offset, local, weight_ref, *refs):
    *h_refs, out_ref = refs

    def run():
        first = lax.axis_index("tensor") * local + offset
        products(h_refs, range(len(h_refs)), weight_ref, first, out_ref)

    when_section(active, run)


def combine_kernel(active, offset, count, chunks, *refs):
    g_refs, refs = refs[:chunks], refs[chunks:]
    own_ref, down_ref = refs[:2]
    inner_refs = refs[2 : 2 + count]
    cross_refs = refs[2 + count : 1 + 2 * count]
    kept_refs, out_ref = refs[1 + 2 * count : -1], refs[-1]
    rows = out_ref.shape[0]

    def run():
        inner = sum(unpack_inner(ref, rows).astype(jnp.float32) for ref in inner_refs)
        inner = inner.astype(jnp.bfloat16)
        width = g_refs[0].shape[1]
        for k, g_ref in enumerate(g_refs):
            at = slice(k * width, (k + 1) * width)
            value = g_ref[...].astype(jnp.float32) + own_ref[:, at].astype(jnp.float32)
            for ref in cross_refs:
                value = value + ref[:rows, at].astype(jnp.float32)
            value = value + ADAPTER_SCALE * lax.dot_general(
                inner,
                down_ref[:, offset + k * width : offset + (k + 1) * width],
                CONTRACT_FIRST,
                preferred_element_type=jnp.float32,
            )
            out_ref[:, at] = value.astype(jnp.bfloat16)

    def keep():
        for k, kept_ref in enumerate(kept_refs):
            width = kept_ref.shape[1]
            out_ref[:, k * width : (k + 1) * width] = kept_ref[...]

    when_section(active, run, keep if kept_refs else None)


def split_rows(total, keep, keep_ref, send_ref):
    half = keep_ref.shape[0]
    first, second = total[:half, :], total[half:, :]
    keep_ref[...] = jnp.where(keep == 0, first, second)
    send_ref[...] = jnp.where(keep == 0, second, first).astype(send_ref.dtype)


def adapter_kernel(factor, count, chunks, replicas, *refs):
    stored_ref, saved_ref = refs[:2]
    h_refs = refs[2 : 2 + chunks]
    inner_refs = refs[2 + chunks : 2 + chunks + count]
    out_refs = refs[2 + chunks + count :]
    inner = sum(ref[...].astype(jnp.float32) for ref in inner_refs).astype(jnp.bfloat16)
    down = factor * jnp.dot(inner, stored_ref[...], preferred_element_type=jnp.float32)
    ups = [
        factor * jnp.dot(saved_ref[...], h_ref[...], preferred_element_type=jnp.float32)
        for h_ref in h_refs
    ]
    total = jnp.concatenate([down, jnp.concatenate(ups, axis=1)], axis=0)
    if len(out_refs) == 2:
        split_rows(total, lax.axis_index("dp") // (replicas // 2), *out_refs)
    else:
        out_refs[0][...] = total.astype(jnp.bfloat16)


def fold_kernel(step, kept_ref, received_ref, keep_ref, send_ref):
    total = kept_ref[...] + received_ref[...].astype(jnp.float32)
    split_rows(total, (lax.axis_index("dp") // step) % 2, keep_ref, send_ref)


def shards(
    query_embedded,
    passage_embedded,
    positives,
    counts,
    stored_inputs,
    adapter_inner,
    branch_slope,
    frozen_projection,
    adapter_down,
    adapter_up,
):
    sizes = tuple(lax.axis_size(name) for name in AXES)
    section_count, replica_total, tensor_count = sizes
    few_replicas = replica_total <= 4
    weight, down, up = frozen_projection[0], adapter_down[0].T, adapter_up[0]
    stored, saved, slope = stored_inputs[0], adapter_inner[0].T, branch_slope[0]
    rows, local = slope.shape
    rank = up.shape[0]
    span = local // CHUNKS
    others = range(1, tensor_count)
    struct = lambda n, kind=jnp.bfloat16: jax.ShapeDtypeStruct((rows, n), kind)
    inner_shape = jax.ShapeDtypeStruct((rank, rows), jnp.bfloat16)
    matmul_flops = lambda depth, columns: 2 * rows * depth * columns

    if (section_count, replica_total) == (4, 4):
        bases = [0, 1, 2, 3]
        pieces = gather_pieces(passage_embedded, sizes)
    else:
        bases = [None]
        pieces = [lax.all_gather(passage_embedded, "dp", axis=0, tiled=True)]
    pitch = -(-pieces[0].shape[0] // 16) * 16
    scale, at = vmem_call(
        setup_kernel,
        (
            struct(128, jnp.float32),
            jax.ShapeDtypeStruct((query_embedded.shape[0], 128), jnp.int32),
        ),
        (positives, counts),
        COVER_FLOPS,
        smem=(0, 1),
    )
    tops = vmem_call(
        functools.partial(top_kernel, len(pieces), bases),
        (struct(span),) * (2 * CHUNKS),
        (scale, at, query_embedded, *pieces, slope),
        0,
        scratch=[pltpu.VMEM((len(pieces) * pitch, passage_embedded.shape[1]), jnp.bfloat16)],
    )
    g, h = tops[:CHUNKS], tops[CHUNKS:]
    inner = None
    results = None
    for active in range(section_count - 1, -1, -1):
        last = active == 0
        width = local if last else span
        offsets = range(0, local, width)
        received = {}
        payload = jax.ShapeDtypeStruct((rows if last else rows + rank, width), jnp.bfloat16)
        swap = lambda values: [
            exchange(value, split_pairing(active, j), sizes)
            for j, value in zip(others, values)
        ]
        if inner is None:
            inner, *crosses = vmem_call(
                functools.partial(first_cross_kernel, active, CHUNKS, 0, local),
                (inner_shape,) + (payload,) * len(others),
                (up, weight, *h),
                matmul_flops(local, width) * len(others),
            )
            parts, bases_held, cross_h = list(range(CHUNKS)), [], h
        else:
            first_h, *bases_held = vmem_call(
                functools.partial(early_kernel, active),
                (struct(span),) + (struct(local, jnp.float32),) * len(others),
                (g[0], slope, h[0], weight),
                matmul_flops(span, local) * len(others),
            )
            if last:
                second_h, inner = vmem_call(
                    functools.partial(branch_kernel, active),
                    (struct(span), inner_shape),
                    (g[1], slope, up, h[1], inner, first_h),
                    matmul_flops(span, rank),
                )
                crosses = vmem_call(
                    functools.partial(later_cross_kernel, active, len(others), [1], 0, local),
                    (struct(width),) * len(others),
                    (inner, weight, second_h, *bases_held),
                    matmul_flops(span, width) * len(others),
                )
            else:
                second_h, inner, *crosses = vmem_call(
                    functools.partial(next_cross_kernel, active, 1 + len(others)),
                    (struct(span), inner_shape) + (payload,) * len(others),
                    (g[1], slope, up, h[1], inner, weight, first_h, *bases_held),
                    matmul_flops(span, width) * len(others),
                )
            h = [first_h, second_h]
            parts, cross_h = [1], [second_h]
        received[0] = swap(crosses)
        inner_others = received[0]
        if last:
            inner_others = [
                exchange(inner, lambda s, d, t, j=j: (s, d, t ^ j), sizes)
                for j in others
            ]
        for offset in offsets[1:]:
            crosses = vmem_call(
                functools.partial(
                    later_cross_kernel, active, len(others), parts, offset, local
                ),
                (struct(width),) * len(others),
                (crosses[0], weight, *cross_h, *bases_held),
                matmul_flops(span * len(parts), width) * len(others),
            )
            received[offset] = swap(crosses)
        sums, next_g = [], []
        for k, offset in enumerate(offsets):
            (own,) = vmem_call(
                functools.partial(own_kernel, active, offset, local),
                (struct(width),),
                (weight, *h),
                matmul_flops(local, width),
            )
            g_parts = g if last else [g[k]]
            kept = [] if results is None else results if last else [results[k]]
            combine = functools.partial(
                combine_kernel, active, offset, tensor_count, len(g_parts)
            )
            terms = (*g_parts, own, down, inner, *inner_others, *received[offset], *kept)
            (total,) = vmem_call(combine, (struct(width),), terms, matmul_flops(rank, width))
            sums.append(total)
            if not last:
                next_g.append(exchange(total, hop_pairing(active), sizes))
        results, g = sums, next_g

    factor = ADAPTER_SCALE / (query_embedded.shape[0] * replica_total)
    halves = lambda n: (
        jax.ShapeDtypeStruct((n, local), jnp.float32),
        jax.ShapeDtypeStruct((n, local), jnp.bfloat16),
    )
    parts = vmem_call(
        functools.partial(adapter_kernel, factor, tensor_count, CHUNKS, replica_total),
        halves(rank) if few_replicas else halves(2 * rank)[1:],
        (stored, saved, *h, inner, *inner_others),
        4 * rows * local * rank,
    )
    if few_replicas:
        kept, sent = parts
        step = replica_total // 2
        while True:
            arrived = exchange(sent, lambda s, d, t, j=step: (s, d ^ j, t), sizes)
            if step == 1:
                break
            step //= 2
            kept, sent = vmem_call(
                functools.partial(fold_kernel, step), halves(kept.shape[0] // 2), (kept, arrived), 0
            )
        reduced = kept + arrived.astype(jnp.float32)
    else:
        reduced = lax.psum_scatter(parts[0], "dp", scatter_dimension=0, tiled=True).astype(
            jnp.float32
        )
    return (results[0][None], reduced[None])


def solution(mesh):
    return jax.shard_map(
        shards,
        mesh=mesh,
        in_specs=(
            P("dp", None),
            P("dp", None),
            P("dp"),
            P("dp"),
            P("section", "dp", "tensor"),
            P("section", "dp", None),
            P("section", "dp", "tensor"),
            P("section", None, "tensor"),
            P("section", "tensor", None),
            P("section", None, "tensor"),
        ),
        out_specs=(P("section", "dp", "tensor"), P("section", "dp", "tensor")),
        check_vma=False,
    )
```
